128 devices in a mesh: basis: 64 (over z, y, x), ex: 2 (over core).
Axes of the slice: x: 4, y: 4, z: 4, core: 2. Of those that a mesh axis runs over, the one named last changes fastest.
Arguments:
- activations: bfloat16 [256, 768, 2880], P(('basis', 'ex')), may hold values from -6 to 6
- out_grads: bfloat16 [256, 768, 2880], P(('basis', 'ex')), may hold values from -0.25 to 0.25
- grad_basis: bfloat16 [2880, 256], replicated, may hold values from -0.109375 to 0.109375
- panel_store: bfloat16 [64, 4, 2880, 128], P('basis', None, 'ex'), may hold values from -0.109375 to 0.109375
- owners: int32 [4], replicated, may hold values from 0 to 63, as said below
- token_count: int32 [256], P(('basis', 'ex')), may hold values from 96 to 768, as said below
Outputs:
- scaled: float32 [256, 256, 512], P('basis', 'ex')
The draws below stay inside these ranges and needn't reach their ends.
Inputs may be any that keep to these rules, and one draw needn't show every extreme that they name: `owners`: values are basis indices; panels may share an owner. `token_count`: some example has all 768 tokens live.
All inputs are finite; a program needn't handle non-finite values.
Results may differ from the reference program's by a relative error of at most 0.00045.
The reference program's roundings to bfloat16 on the way (of `in_basis`, `rot_act` and `rot_grad`) count: a program that leaves them out, or rounds other values in their place, can miss the bound.
Values may be sent and summed in bfloat16 or wider, within the bound.
No kernel may reach another device: no remote copies, remote signals or barrier semaphores. Data moves between devices by JAX's collectives and lax.ppermute only.
A program may use at most 128 MiB of HBM per device.

```python
import jax
import jax.numpy as jnp
from jax import lax

D_IN = 2880
D_OUT = 2880
TOK = 768
PANEL = 128
PANELS = 4
DIRS = 256
EXAMPLES = 256
N_BASIS = 64


def draw_owners(key, part):
    first, second = jax.random.split(jax.random.fold_in(key, 11))
    picks = jax.random.randint(first, (PANELS,), 0, N_BASIS)
    picks = picks.at[0].set(0).at[1].set(N_BASIS - 1)
    return jax.random.permutation(second, picks).astype(jnp.int32)


def draw_token_count(key, part):
    first, second = jax.random.split(jax.random.fold_in(key, 23))
    counts = jax.random.randint(first, (EXAMPLES,), TOK // 8, TOK + 1)
    target = jax.random.randint(second, (), 0, EXAMPLES)
    return counts.at[target].set(TOK).astype(jnp.int32)


def steps_of(stream_key, dims, cuts, low, largest):
    def one(axis_at, shards_of):
        heights = jax.random.uniform(jax.random.fold_in(jax.random.fold_in(stream_key, 6), axis_at), (shards_of,), jnp.float32, low / len(cuts), largest / len(cuts))
        return jnp.repeat(jnp.exp(heights), dims[axis_at] // shards_of).reshape((-1,) + (1,) * (len(dims) - axis_at - 1))

    gain = one(*cuts[0])
    for cut in cuts[1:]:
        gain = gain * one(*cut)
    return gain


def normal_values(rng, shape, deviation, limit, cuts=(), dtype=jnp.bfloat16):
    result = deviation * jax.random.normal(rng, shape, jnp.float32)
    if cuts:
        result = result * steps_of(rng, shape, cuts, -0.22, 0.18)
    return jnp.clip(result, -limit, limit).astype(dtype)


def setup_inputs(seed: int = 0) -> dict:
    streams_of = jax.random.split(jax.random.key(seed), 7)
    activations = normal_values(streams_of[0], (EXAMPLES, TOK, D_IN), 1.0, 6.0, ((0, 128),))
    out_grads = normal_values(streams_of[1], (EXAMPLES, TOK, D_OUT), 0.036, 0.25, ((0, 128),))
    grad_basis = normal_values(streams_of[2], (D_OUT, DIRS), D_OUT ** -0.5, 0.109375)
    panel_store = normal_values(streams_of[3], (N_BASIS, PANELS, D_IN, PANEL), D_IN ** -0.5, 0.109375, ((0, 64), (2, 2)))
    owners = draw_owners(jax.random.fold_in(streams_of[6], 71), 0)
    token_count = draw_token_count(jax.random.fold_in(streams_of[6], 71), 0)
    return {"activations": activations, "out_grads": out_grads, "grad_basis": grad_basis, "panel_store": panel_store, "owners": owners, "token_count": token_count}


def reference(activations, out_grads, grad_basis, panel_store, owners, token_count):
    picked = panel_store[owners, jnp.arange(PANELS)]
    in_basis = jnp.transpose(picked, (1, 0, 2)).reshape(D_IN, PANELS * PANEL)
    positions = jnp.arange(TOK)

    def one_example(inputs):
        act_rows, grad_rows, length = inputs
        rot_act = jnp.dot(act_rows, in_basis, preferred_element_type=jnp.float32).astype(jnp.bfloat16)
        rot_grad = jnp.dot(grad_rows, grad_basis, preferred_element_type=jnp.float32).astype(jnp.bfloat16)
        rot_grad = jnp.where((positions < length)[:, None], rot_grad, jnp.zeros((), jnp.bfloat16))
        return jnp.dot(rot_grad.T, rot_act, preferred_element_type=jnp.float32)

    ex_grads = lax.map(one_example, (activations, out_grads, token_count))
    lambdas = jnp.sum(ex_grads * ex_grads, axis=0) / EXAMPLES
    damp = 0.1 * jnp.mean(lambdas)
    return ex_grads / (lambdas + damp)
```

```python
import functools

import jax
import jax.numpy as jnp
from jax import lax
from jax.experimental import pallas as pl
from jax.experimental.pallas import tpu as pltpu
from jax.sharding import PartitionSpec as P

ROWS = 96
TT = 256
F32 = jnp.float32
BF16 = jnp.bfloat16


def grads_kernel(e_ref, act_ref, rg_ref, mine_ref, other_ref, keep_ref, send_ref, sq_ref, basis, acc, sq, sems):
    n, t = pl.program_id(0), pl.program_id(1)
    nt = pl.num_programs(1)
    e = e_ref[0]
    half = basis.shape[0] // 2
    panels = basis.shape[1] // 128

    def copies():
        out = []
        for h, src in enumerate((mine_ref, other_ref)):
            at = pl.multiple_of((e if h == 0 else 1 - e) * half, 16)
            for k in range(panels):
                out.append(
                    pltpu.make_async_copy(
                        src.at[pl.ds(k * half, half), :],
                        basis.at[pl.ds(at, half), pl.ds(k * 128, 128)],
                        sems.at[h * panels + k],
                    )
                )
        return out

    @pl.when((n == 0) & (t == 0))
    def _():
        for c in copies():
            c.start()
        for c in copies():
            c.wait()
        sq[...] = jnp.zeros_like(sq)

    rot = jnp.dot(act_ref[0], basis[...], preferred_element_type=F32).astype(BF16)
    part = jnp.dot(rg_ref[0], rot, preferred_element_type=F32)

    @pl.when(t == 0)
    def _():
        acc[...] = part

    @pl.when(t > 0)
    def _():
        acc[...] += part

    @pl.when(t == nt - 1)
    def _():
        dirs = acc.shape[0] // 2
        keep_ref[0] = acc[pl.ds(pl.multiple_of(e * dirs, 8), dirs), :]
        send_ref[0] = acc[pl.ds(pl.multiple_of((1 - e) * dirs, 8), dirs), :]
        sq[...] += acc[...] * acc[...]

    @pl.when((t == nt - 1) & (n == pl.num_programs(0) - 1))
    def _():
        dirs = acc.shape[0] // 2
        cols = acc.shape[1] // 128
        for h in range(2):
            for r in range(dirs // 8):
                for c in range(cols):
                    sq_ref[2 * (cols * r + c) + h] = sq[pl.ds(h * dirs + 8 * r, 8), pl.ds(128 * c, 128)]


def ex_gradients(e, act, rg, mine, other):
    local, tok, width = act.shape
    dirs = rg.shape[1]
    half = width // 2
    cols = mine.shape[0] // half * 128
    grid = (local, tok // TT)
    return pl.pallas_call(
        grads_kernel,
        grid_spec=pltpu.PrefetchScalarGridSpec(
            num_scalar_prefetch=1,
            grid=grid,
            in_specs=[
                pl.BlockSpec((1, TT, width), lambda n, t, e: (n, t, 0)),
                pl.BlockSpec((1, dirs, TT), lambda n, t, e: (n, 0, t)),
                pl.BlockSpec(memory_space=pl.ANY),
                pl.BlockSpec(memory_space=pl.ANY),
            ],
            out_specs=[
                pl.BlockSpec((1, dirs // 2, cols), lambda n, t, e: (n, 0, 0)),
                pl.BlockSpec((1, dirs // 2, cols), lambda n, t, e: (n, 0, 0)),
                pl.BlockSpec((dirs * cols // 1024, 8, 128), lambda n, t, e: (0, 0, 0)),
            ],
            scratch_shapes=[
                pltpu.VMEM((width, cols), BF16),
                pltpu.VMEM((dirs, cols), F32),
                pltpu.VMEM((dirs, cols), F32),
                pltpu.SemaphoreType.DMA((2 * (cols // 128),)),
            ],
        ),
        out_shape=[
            jax.ShapeDtypeStruct((local, dirs // 2, cols), F32),
            jax.ShapeDtypeStruct((local, dirs // 2, cols), F32),
            jax.ShapeDtypeStruct((dirs * cols // 1024, 8, 128), F32),
        ],
        compiler_params=pltpu.CompilerParams(vmem_limit_bytes=40 << 20),
    )(e, act, rg, mine, other)


def lambda_kernel(scale, x_ref, o_ref):
    lam = jnp.sum(x_ref[...], axis=0) * scale
    o_ref[...] = jnp.broadcast_to(lam[None], o_ref.shape)


def scale_kernel(e_ref, lam_ref, keep_ref, got_ref, o_ref):
    e = e_ref[0]
    local, dirs, cols = keep_ref.shape
    tiles = lam_ref.shape[0] // 2
    damp = jnp.sum(jnp.sum(lam_ref[...], axis=0), keepdims=True) * (0.1 / (lam_ref.size))
    across = cols // 128
    for i in range(tiles):
        r, c = i // across, i % across
        at = (slice(8 * r, 8 * r + 8), slice(128 * c, 128 * c + 128))
        inv = 1.0 / (lam_ref[2 * i + e] + damp)
        for j in range(local):
            o_ref[e * local + j, at[0], at[1]] = keep_ref[j, at[0], at[1]] * inv
            o_ref[(1 - e) * local + j, at[0], at[1]] = got_ref[j, at[0], at[1]] * inv


def per_device(activations, out_grads, grad_basis, panel_store, owners, token_count):
    local, tok, width = activations.shape
    _, panels, half, pw = panel_store.shape
    n_basis, n_ex = lax.axis_size("basis"), lax.axis_size("ex")
    b, e = lax.axis_index("basis"), lax.axis_index("ex")
    both = ("basis", "ex")
    e1 = e.reshape(1).astype(jnp.int32)

    blocks = half // ROWS
    slots = panel_store.reshape(panels * blocks, ROWS, pw)
    spare = n_basis - panels * blocks
    slots = jnp.concatenate([slots, slots[:spare]], axis=0)
    arrived = lax.all_to_all(slots, "basis", 0, 0, tiled=True)
    owner = owners[jnp.minimum(b // blocks, panels - 1)]
    block = lax.dynamic_index_in_dim(arrived, owner, 0, keepdims=True)
    spread = jnp.broadcast_to(block, arrived.shape)
    mine = lax.all_to_all(spread, "basis", 0, 0, tiled=True).reshape(n_basis * ROWS, pw)
    swap = [(0, 1), (1, 0)]
    other = lax.ppermute(mine, "ex", swap)

    rg = lax.dot_general(grad_basis, out_grads, (((0,), (2,)), ((), ())), preferred_element_type=F32)
    rg = jnp.transpose(rg, (1, 0, 2)).astype(BF16)
    live = jnp.arange(tok)[None, :] < token_count[:, None]
    rg = jnp.where(live[:, None, :], rg, jnp.zeros((), BF16))

    keep, send, squares = ex_gradients(e1, activations, rg, mine, other)
    got = lax.ppermute(send, "ex", swap)
    ex_count = local * n_basis * n_ex
    parts = lax.all_to_all(squares, both, 0, 0, tiled=True)
    lam = pl.pallas_call(
        functools.partial(lambda_kernel, 1.0 / ex_count),
        out_shape=jax.ShapeDtypeStruct(parts.shape, F32),
    )(parts)
    lam = lax.all_to_all(lam, both, 0, 0, tiled=True)
    return pl.pallas_call(
        scale_kernel,
        in_specs=[pl.BlockSpec(memory_space=pltpu.SMEM)] + [pl.BlockSpec(memory_space=pltpu.VMEM)] * 3,
        out_shape=jax.ShapeDtypeStruct((2 * local, keep.shape[1], keep.shape[2]), F32),
    )(e1, lam, keep, got)


def solution(mesh):
    return jax.shard_map(
        per_device,
        mesh=mesh,
        in_specs=(
            P(("basis", "ex"), None, None),
            P(("basis", "ex"), None, None),
            P(),
            P("basis", None, "ex", None),
            P(),
            P(("basis", "ex")),
        ),
        out_specs=P("basis", "ex", None),
        check_vma=False,
    )
```

```python
import jax
import jax.numpy as jnp
from jax import lax
from jax.experimental import pallas as pl
from jax.experimental.pallas import tpu as pltpu
from jax.sharding import PartitionSpec as P

ROWS = 96
TT = 256
F32 = jnp.float32
BF16 = jnp.bfloat16


def turn_kernel(e_ref, x_ref, o_ref):
    o_ref[0, 0] = x_ref[0].T


def turned(e, activations):
    local, tok, width = activations.shape
    half = width // 2
    return pl.pallas_call(
        turn_kernel,
        grid_spec=pltpu.PrefetchScalarGridSpec(
            num_scalar_prefetch=1,
            grid=(2, local, tok // TT),
            in_specs=[pl.BlockSpec((1, half, TT), lambda h, n, t, e: (n, h + e[0] - 2 * h * e[0], t))],
            out_specs=pl.BlockSpec((1, 1, TT, half), lambda h, n, t, e: (h, n, t, 0)),
        ),
        out_shape=pltpu.HBM((2, local, tok, half), BF16),
        compiler_params=pltpu.CompilerParams(vmem_limit_bytes=24 << 20),
        cost_estimate=pl.CostEstimate(flops=0, transcendentals=0, bytes_accessed=4 * local * tok * width),
    )(e, pltpu.with_memory_space_constraint(jnp.swapaxes(activations, 1, 2), pltpu.HBM))


def half_product(act, basis_ref, half, p):
    pair = jnp.concatenate([basis_ref[pl.ds(k * half, half), :] for k in (p, p + 1)], axis=1)
    return jnp.dot(act, pair, preferred_element_type=F32)


def first_kernel(act_ref, basis_ref, o_ref):
    act = act_ref[0, 0]
    half = act.shape[1]
    for p in range(0, o_ref.shape[2] // 128, 2):
        o_ref[0, :, pl.ds(p * 128, 256)] = half_product(act, basis_ref, half, p)


def second_kernel(e_ref, act_ref, rg_ref, first_ref, basis_ref, keep_ref, send_ref, sq_ref, acc, sq):
    n, t = pl.program_id(0), pl.program_id(1)
    nt = pl.num_programs(1)
    e = e_ref[0]
    act = act_ref[0, 0]
    half = act.shape[1]
    for p in range(0, acc.shape[1] // 128, 2):
        at = pl.ds(p * 128, 256)
        rot = (first_ref[0, :, at] + half_product(act, basis_ref, half, p)).astype(BF16)
        part = jnp.dot(rg_ref[0], rot, preferred_element_type=F32)
        acc[:, at] = jnp.where(t == 0, part, acc[:, at] + part)

    @pl.when(t == nt - 1)
    def _():
        dirs = acc.shape[0] // 2
        keep_ref[0] = acc[pl.ds(pl.multiple_of(e * dirs, 8), dirs), :]
        send_ref[0] = acc[pl.ds(pl.multiple_of((1 - e) * dirs, 8), dirs), :]

    @pl.when((t == nt - 1) & (n == 0))
    def _():
        sq[...] = acc[...] * acc[...]

    @pl.when((t == nt - 1) & (n > 0))
    def _():
        sq[...] += acc[...] * acc[...]

    @pl.when((t == nt - 1) & (n == pl.num_programs(0) - 1))
    def _():
        dirs = acc.shape[0] // 2
        cols = acc.shape[1] // 128
        for h in range(2):
            for r in range(dirs // 8):
                for c in range(cols):
                    sq_ref[2 * (cols * r + c) + h] = sq[pl.ds(h * dirs + 8 * r, 8), pl.ds(128 * c, 128)]


def first_half(act, mine, panels):
    _, local, tok, half = act.shape
    cols = panels * 128
    return pl.pallas_call(
        first_kernel,
        grid=(local, tok // TT),
        in_specs=[
            pl.BlockSpec((1, 1, TT, half), lambda n, t: (0, n, t, 0)),
            pl.BlockSpec((panels * half, 128), lambda n, t: (0, 0)),
        ],
        out_specs=pl.BlockSpec((1, TT, cols), lambda n, t: (n, t, 0)),
        out_shape=jax.ShapeDtypeStruct((local, tok, cols), F32),
        compiler_params=pltpu.CompilerParams(vmem_limit_bytes=24 << 20),
        cost_estimate=pl.CostEstimate(
            flops=2 * local * tok * half * cols, transcendentals=0, bytes_accessed=2 * local * tok * half
        ),
    )(pltpu.with_memory_space_constraint(act, pltpu.HBM), mine)


def ex_gradients(e, act, rg, first, other):
    _, local, tok, half = act.shape
    dirs, cols = rg.shape[1], first.shape[2]
    panels = cols // 128
    return pl.pallas_call(
        second_kernel,
        grid_spec=pltpu.PrefetchScalarGridSpec(
            num_scalar_prefetch=1,
            grid=(local, tok // TT),
            in_specs=[
                pl.BlockSpec((1, 1, TT, half), lambda n, t, e: (1, n, t, 0)),
                pl.BlockSpec((1, dirs, TT), lambda n, t, e: (n, 0, t)),
                pl.BlockSpec((1, TT, cols), lambda n, t, e: (n, t, 0)),
                pl.BlockSpec((panels * half, 128), lambda n, t, e: (0, 0)),
            ],
            out_specs=[
                pl.BlockSpec((1, dirs // 2, cols), lambda n, t, e: (n, 0, 0)),
                pl.BlockSpec((1, dirs // 2, cols), lambda n, t, e: (n, 0, 0)),
                pl.BlockSpec((dirs * cols // 1024, 8, 128), lambda n, t, e: (0, 0, 0)),
            ],
            scratch_shapes=[pltpu.VMEM((dirs, cols), F32), pltpu.VMEM((dirs, cols), F32)],
        ),
        out_shape=[
            pltpu.HBM((local, dirs // 2, cols), F32),
            pltpu.HBM((local, dirs // 2, cols), F32),
            pltpu.HBM((dirs * cols // 1024, 8, 128), F32),
        ],
        compiler_params=pltpu.CompilerParams(vmem_limit_bytes=32 << 20),
        cost_estimate=pl.CostEstimate(
            flops=2 * local * tok * half * cols, transcendentals=0, bytes_accessed=2 * local * tok * half
        ),
    )(e, pltpu.with_memory_space_constraint(act, pltpu.HBM), rg, first, other)


def scale_kernel(e_ref, lam_ref, keep_ref, got_ref, o_ref, inv):
    e, i = e_ref[0], pl.program_id(0)
    local, dirs, cols = keep_ref.shape
    tiles, across = lam_ref.shape[0] // 2, cols // 128

    @pl.when(i == 0)
    def _():
        damp = jnp.sum(jnp.sum(lam_ref[...], axis=0), keepdims=True) * (0.1 / lam_ref.size)
        for j in range(tiles):
            r, c = j // across, j % across
            inv[pl.ds(8 * r, 8), pl.ds(128 * c, 128)] = 1.0 / (lam_ref[2 * j + e] + damp)

    for core in range(2):
        for j in range(local):
            for own in range(2):

                @pl.when((i == core * local + j) & (own == (e == core)))
                def _():
                    src = keep_ref if own else got_ref
                    o_ref[0] = src[j] * inv[...]


def scaled_rows(e, lam, keep, got):
    local, dirs, cols = keep.shape

    def whole(x):
        return pl.BlockSpec(x.shape, lambda i, e: (0, 0, 0))

    return pl.pallas_call(
        scale_kernel,
        grid_spec=pltpu.PrefetchScalarGridSpec(
            num_scalar_prefetch=1,
            grid=(2 * local,),
            in_specs=[whole(lam), whole(keep), whole(got)],
            out_specs=pl.BlockSpec((1, dirs, cols), lambda i, e: (i, 0, 0)),
            scratch_shapes=[pltpu.VMEM((dirs, cols), F32)],
        ),
        out_shape=jax.ShapeDtypeStruct((2 * local, dirs, cols), F32),
        compiler_params=pltpu.CompilerParams(vmem_limit_bytes=8 << 20),
    )(e, lam, keep, got)


def per_device(activations, out_grads, grad_basis, panel_store, owners, token_count):
    local, tok, width = activations.shape
    _, panels, half, pw = panel_store.shape
    n_basis, n_ex = lax.axis_size("basis"), lax.axis_size("ex")
    b, e = lax.axis_index("basis"), lax.axis_index("ex")
    both = ("basis", "ex")
    e1 = e.reshape(1).astype(jnp.int32)

    blocks = half // ROWS
    slots = panel_store.reshape(panels * blocks, ROWS, pw)
    slots = jnp.pad(slots, ((0, n_basis - panels * blocks), (0, 0), (0, 0)))
    arrived = lax.all_to_all(slots, "basis", 0, 0, tiled=True)
    act = turned(e1, activations)
    arrived, act = lax.optimization_barrier((arrived, act))

    owner = owners[jnp.minimum(b // blocks, panels - 1)]
    block = lax.dynamic_index_in_dim(arrived, owner, 0, keepdims=True)
    spread = jnp.broadcast_to(block, arrived.shape)
    mine = lax.all_to_all(spread, "basis", 0, 0, tiled=True)

    rg = lax.dot_general(grad_basis, out_grads, (((0,), (2,)), ((), ())), preferred_element_type=F32)
    rg = jnp.transpose(rg, (1, 0, 2)).astype(BF16)
    live = jnp.arange(tok)[None, :] < token_count[:, None]
    rg = jnp.where(live[:, None, :], rg, jnp.zeros((), BF16))
    mine, rg = lax.optimization_barrier((mine, rg))

    mine = mine.reshape(n_basis * ROWS, pw)
    swap = [(0, 1), (1, 0)]
    other = lax.ppermute(mine, "ex", swap)
    first = first_half(act, mine, panels)
    keep, send, squares = ex_gradients(e1, act, rg, first, other)
    got = lax.ppermute(send, "ex", swap)
    parts = lax.all_to_all(squares, both, 0, 0, tiled=True)
    lam = jnp.sum(parts, axis=0, keepdims=True) * (1.0 / (local * n_basis * n_ex))
    lam = lax.all_to_all(jnp.broadcast_to(lam, parts.shape), both, 0, 0, tiled=True)
    return scaled_rows(e1, lam, keep, got)


def solution(mesh):
    return jax.shard_map(
        per_device,
        mesh=mesh,
        in_specs=(
            P(("basis", "ex"), None, None),
            P(("basis", "ex"), None, None),
            P(),
            P("basis", None, "ex", None),
            P(),
            P(("basis", "ex")),
        ),
        out_specs=P("basis", "ex", None),
        check_vma=False,
    )
```

```python
import jax
import jax.numpy as jnp
from jax import lax
from jax.experimental import pallas as pl
from jax.experimental.pallas import tpu as pltpu
from jax.sharding import PartitionSpec as P

ROWS = 48
TT = 256
HALF = 1440
F32 = jnp.float32
BF16 = jnp.bfloat16


def in_vmem(n):
    return [pl.BlockSpec(memory_space=pltpu.VMEM)] * n


def turn_kernel(x_ref, o_ref):
    o_ref[0] = x_ref[0].T


def turned(activations):
    local, tok, width = activations.shape
    x = pltpu.with_memory_space_constraint(jnp.swapaxes(activations, 1, 2), pltpu.HBM)
    return pl.pallas_call(
        turn_kernel,
        grid=(local,),
        in_specs=[pl.BlockSpec((1, width, tok), lambda n: (n, 0, 0))],
        out_specs=pl.BlockSpec((1, tok, width), lambda n: (n, 0, 0)),
        out_shape=pltpu.HBM((local, tok, width), BF16),
        compiler_params=pltpu.CompilerParams(vmem_limit_bytes=28 << 20),
        cost_estimate=pl.CostEstimate(flops=0, transcendentals=0, bytes_accessed=4 * local * tok * width),
    )(x)


def pair_of_panels(ref):
    half = HALF
    blocks = half // ROWS
    cols = []
    for k in range(2):
        rows = [ref[pl.ds(k * blocks, blocks), h].reshape(half, 128) for h in range(2)]
        cols.append(jnp.concatenate(rows, axis=0))
    return jnp.concatenate(cols, axis=1)


def pair_products(act_ref, rg_ref, basis_ref, rot):
    local, tok, _ = act_ref.shape
    pair = pair_of_panels(basis_ref)
    for n in range(local):
        for t in range(0, tok, TT):
            rows = pl.ds(t, TT)
            rot[n, rows] = jnp.dot(act_ref[n, rows], pair, preferred_element_type=F32).astype(BF16)
    return [jnp.dot(rg_ref[n], rot[n], preferred_element_type=F32) for n in range(local)]


def first_kernel(act_ref, rg_ref, basis_ref, ex_ref, rot):
    for n, ex in enumerate(pair_products(act_ref, rg_ref, basis_ref, rot)):
        ex_ref[n] = ex


def second_kernel(e_ref, act_ref, rg_ref, basis_ref, own_ref, keep_ref, send_ref, sq_ref, rot, ex_ref, sq):
    e = e_ref[0]
    local, dirs, cols = own_ref.shape
    mid = dirs // 2
    for n, ex in enumerate(pair_products(act_ref, rg_ref, basis_ref, rot)):
        ex_ref[n] = ex
    here, there = (pl.ds(pl.multiple_of(x * mid, 8), mid) for x in (e, 1 - e))
    for n in range(local):
        for side, src in enumerate((own_ref, ex_ref)):
            keep_ref[n, side] = src[n, here, :]
            send_ref[n, side] = src[n, there, :]
    for side, src in enumerate((own_ref, ex_ref)):
        pair = e if side == 0 else 1 - e
        for h in range(2):
            for r in range(mid // 8):
                for c in range(cols // 128):
                    at = (pl.ds(h * mid + 8 * r, 8), pl.ds(128 * c, 128))
                    tile = src[0, at[0], at[1]] * src[0, at[0], at[1]]
                    for n in range(1, local):
                        tile += src[n, at[0], at[1]] * src[n, at[0], at[1]]
                    sq_ref[2 * (2 * (cols // 128) * r + (cols // 128) * pair + c) + h] = tile


def ex_gradients(e, act, rg, mine, other):
    local, tok, width = act.shape
    dirs = rg.shape[1]
    cost = pl.CostEstimate(
        flops=2 * local * tok * width * 256, transcendentals=0, bytes_accessed=2 * local * tok * width
    )
    own = pl.pallas_call(
        first_kernel,
        in_specs=in_vmem(3),
        out_specs=pl.BlockSpec(memory_space=pltpu.VMEM),
        out_shape=pltpu.VMEM((local, dirs, 256), F32),
        scratch_shapes=[pltpu.VMEM((local, tok, 256), BF16)],
        compiler_params=pltpu.CompilerParams(vmem_limit_bytes=16 << 20),
        cost_estimate=cost,
    )(act, rg, mine)
    return pl.pallas_call(
        second_kernel,
        in_specs=[pl.BlockSpec(memory_space=pltpu.SMEM)] + in_vmem(4),
        out_specs=in_vmem(3),
        out_shape=[
            pltpu.HBM((local, 2, dirs // 2, 256), F32),
            pltpu.HBM((local, 2, dirs // 2, 256), F32),
            pltpu.HBM((dirs * 512 // 1024, 8, 128), F32),
        ],
        scratch_shapes=[
            pltpu.VMEM((local, tok, 256), BF16),
            pltpu.VMEM((local, dirs, 256), F32),
            pltpu.VMEM((dirs, 256), F32),
        ],
        compiler_params=pltpu.CompilerParams(vmem_limit_bytes=16 << 20),
        cost_estimate=cost,
    )(e, act, rg, other, own)


def scale_kernel(e_ref, lam_ref, keep_ref, got_ref, o_ref, inv):
    e, i = e_ref[0], pl.program_id(0)
    local = keep_ref.shape[0]
    tiles, across = lam_ref.shape[0] // 2, 4

    @pl.when(i == 0)
    def _():
        damp = jnp.sum(jnp.sum(lam_ref[...], axis=0), keepdims=True) * (0.1 / lam_ref.size)
        for j in range(tiles):
            r, c = j // across, j % across
            inv[pl.ds(8 * r, 8), pl.ds(128 * c, 128)] = 1.0 / (lam_ref[2 * j + e] + damp)

    for core in range(2):
        for j in range(local):
            for own in range(2):

                @pl.when((i == core * local + j) & (own == (e == core)))
                def _():
                    src = keep_ref if own else got_ref
                    for side in range(2):
                        at = pl.ds(256 * (core if side == 0 else 1 - core), 256)
                        o_ref[0, :, at] = src[j, side] * inv[:, at]


def scaled_rows(e, lam, keep, got):
    local, _, dirs, _ = keep.shape

    def whole(x):
        return pl.BlockSpec(x.shape, lambda i, e: (0,) * x.ndim)

    return pl.pallas_call(
        scale_kernel,
        grid_spec=pltpu.PrefetchScalarGridSpec(
            num_scalar_prefetch=1,
            grid=(2 * local,),
            in_specs=[whole(lam), whole(keep), whole(got)],
            out_specs=pl.BlockSpec((1, dirs, 512), lambda i, e: (i, 0, 0)),
            scratch_shapes=[pltpu.VMEM((dirs, 512), F32)],
        ),
        out_shape=jax.ShapeDtypeStruct((2 * local, dirs, 512), F32),
        compiler_params=pltpu.CompilerParams(vmem_limit_bytes=8 << 20),
    )(e, lam, keep, got)


def per_device(activations, out_grads, grad_basis, panel_store, owners, token_count):
    local, tok, width = activations.shape
    _, panels, half, pw = panel_store.shape
    n_basis, n_ex = lax.axis_size("basis"), lax.axis_size("ex")
    b, e = lax.axis_index("basis"), lax.axis_index("ex")
    e1 = e.reshape(1).astype(jnp.int32)
    blocks = half // ROWS
    pairs = panels // 2

    slots = panel_store.reshape(pairs, 2 * blocks, ROWS, pw)
    slots = jnp.pad(slots, ((0, 0), (0, n_basis - 2 * blocks), (0, 0), (0, 0)))
    arrived = lax.all_to_all(slots.reshape(pairs * n_basis, ROWS, pw), ("ex", "basis"), 0, 0, tiled=True)
    act = turned(activations)
    rg = lax.dot_general(grad_basis, out_grads, (((0,), (2,)), ((), ())), preferred_element_type=F32)
    rg = jnp.transpose(rg, (1, 0, 2)).astype(BF16)
    live = jnp.arange(tok)[None, :] < token_count[:, None]
    rg = jnp.where(live[:, None, :], rg, jnp.zeros((), BF16))
    arrived, act, rg = lax.optimization_barrier((arrived, act, rg))

    owner = owners[2 * e + jnp.where(b < blocks, 0, 1)]
    block = lax.dynamic_index_in_dim(arrived.reshape(2, n_basis, ROWS, pw), owner, 1, keepdims=False)
    spread = jnp.broadcast_to(block[None], (n_basis, 2, ROWS, pw))
    mine = lax.all_to_all(spread, "basis", 0, 0, tiled=True)

    swap = [(0, 1), (1, 0)]
    other = lax.ppermute(mine, "ex", swap)
    keep, send, squares = ex_gradients(e1, act, rg, mine, other)
    got = lax.ppermute(send, "ex", swap)
    both = ("basis", "ex")
    parts = lax.all_to_all(squares, both, 0, 0, tiled=True)
    lam = jnp.sum(parts, axis=0, keepdims=True) * (1.0 / (local * n_basis * n_ex))
    lam = lax.all_to_all(jnp.broadcast_to(lam, parts.shape), both, 0, 0, tiled=True)
    return scaled_rows(e1, lam, keep, got)


def solution(mesh):
    return jax.shard_map(
        per_device,
        mesh=mesh,
        in_specs=(
            P(("basis", "ex"), None, None),
            P(("basis", "ex"), None, None),
            P(),
            P("basis", None, "ex", None),
            P(),
            P(("basis", "ex")),
        ),
        out_specs=P("basis", "ex", None),
        check_vma=False,
    )
```

```python
import functools

import jax
import jax.numpy as jnp
from jax import lax
from jax.experimental import pallas as pl
from jax.experimental.pallas import tpu as pltpu
from jax.sharding import PartitionSpec as P

ROWS = 48
TT = 256
HALF = 1440
F32 = jnp.float32
BF16 = jnp.bfloat16


def in_vmem(n):
    return [pl.BlockSpec(memory_space=pltpu.VMEM)] * n


def lay_kernel(cuts, x_ref, o_ref, held, sems):
    pairs, blocks = x_ref.shape[:2]
    step = blocks // cuts
    takes, gives = [], []
    for p in range(pairs):
        for i in range(cuts):
            at = pl.ds(i * step, step)
            k = p * cuts + i
            takes.append(pltpu.make_async_copy(x_ref.at[p, at], held.at[p, at], sems.at[0, k]))
            gives.append(pltpu.make_async_copy(held.at[p, at], o_ref.at[p, at], sems.at[1, k]))
    for c in takes:
        c.start()
    for c, d in zip(takes, gives):
        c.wait()
        d.start()
    for d in gives:
        d.wait()


def laid(slots, n_basis):
    pairs, blocks, rows, width = slots.shape
    cuts = 3
    return pl.pallas_call(
        functools.partial(lay_kernel, cuts),
        in_specs=[pl.BlockSpec(memory_space=pl.ANY)],
        out_specs=pl.BlockSpec(memory_space=pl.ANY),
        out_shape=pltpu.HBM((pairs, n_basis, rows, width), slots.dtype),
        scratch_shapes=[pltpu.VMEM(slots.shape, slots.dtype), pltpu.SemaphoreType.DMA((2, pairs * cuts))],
        compiler_params=pltpu.CompilerParams(vmem_limit_bytes=4 << 20),
    )(pltpu.with_memory_space_constraint(slots, pltpu.HBM))


def turn_kernel(x_ref, *o_refs):
    parts = x_ref.shape[2] // TT
    for i, o_ref in enumerate(o_refs):

        @pl.when(pl.program_id(0) == i // parts)
        def _():
            o_ref[...] = x_ref[0, :, pl.ds(i % parts * TT, TT)].T


def turned(activations):
    local, tok, width = activations.shape
    x = pltpu.with_memory_space_constraint(jnp.swapaxes(activations, 1, 2), pltpu.HBM)
    count = local * tok // TT
    return pl.pallas_call(
        turn_kernel,
        grid=(local,),
        in_specs=[pl.BlockSpec((1, width, tok), lambda n: (n, 0, 0))],
        out_specs=[pl.BlockSpec((TT, width), lambda n: (0, 0))] * count,
        out_shape=[pltpu.HBM((TT, width), BF16)] * count,
        compiler_params=pltpu.CompilerParams(vmem_limit_bytes=40 << 20),
        cost_estimate=pl.CostEstimate(flops=0, transcendentals=0, bytes_accessed=4 * local * tok * width),
    )(x)


def pair_of_panels(ref):
    half = HALF
    blocks = half // ROWS
    cols = []
    for k in range(2):
        rows = [ref[pl.ds(k * blocks, blocks), h].reshape(half, 128) for h in range(2)]
        cols.append(jnp.concatenate(rows, axis=0))
    return jnp.concatenate(cols, axis=1)


def rotate(act_refs, pair, rot, slot):
    for t, act_ref in enumerate(act_refs):
        rot[slot, pl.ds(t * TT, TT)] = jnp.dot(act_ref[...], pair, preferred_element_type=F32).astype(BF16)


def first_kernel(*refs):
    *act_refs, rg_ref, basis_ref, ex_ref, rot = refs
    rotate(act_refs, pair_of_panels(basis_ref), rot, 0)
    ex_ref[...] = jnp.dot(rg_ref[0], rot[0], preferred_element_type=F32)


def second_kernel(e_ref, *refs):
    *act_refs, rg_ref, mine_ref, other_ref, own0_ref, keep_ref, send_ref, sq_ref, rot, own_ref, ex_ref = refs
    e = e_ref[0]
    local, dirs, cols = own_ref.shape
    mid = dirs // 2
    parts = len(act_refs) // local
    rotate(act_refs[parts:], pair_of_panels(mine_ref), rot, 0)
    pair = pair_of_panels(other_ref)
    rotate(act_refs[:parts], pair, rot, 1)
    rotate(act_refs[parts:], pair, rot, 2)
    own_ref[0] = own0_ref[...]
    own_ref[1] = jnp.dot(rg_ref[1], rot[0], preferred_element_type=F32)
    for n in range(local):
        ex_ref[n] = jnp.dot(rg_ref[n], rot[1 + n], preferred_element_type=F32)
    here, there = (pl.ds(pl.multiple_of(x * mid, 8), mid) for x in (e, 1 - e))
    for n in range(local):
        for side, src in enumerate((own_ref, ex_ref)):
            keep_ref[n, side] = src[n, here, :]
            send_ref[n, side] = src[n, there, :]
    for side, src in enumerate((own_ref, ex_ref)):
        pair = e if side == 0 else 1 - e
        for h in range(2):
            for r in range(mid // 8):
                for c in range(cols // 128):
                    at = (pl.ds(h * mid + 8 * r, 8), pl.ds(128 * c, 128))
                    tile = src[0, at[0], at[1]] * src[0, at[0], at[1]]
                    for n in range(1, local):
                        tile += src[n, at[0], at[1]] * src[n, at[0], at[1]]
                    sq_ref[2 * (2 * (cols // 128) * r + (cols // 128) * pair + c) + h] = tile


def ex_gradients(e, act, rg, mine, other):
    local, dirs, tok = rg.shape
    width = act[0].shape[1]
    parts = len(act) // local

    def cost(count):
        return pl.CostEstimate(
            flops=2 * count * tok * width * 256, transcendentals=0, bytes_accessed=2 * count * tok * width
        )

    own = pl.pallas_call(
        first_kernel,
        in_specs=in_vmem(parts + 2),
        out_specs=pl.BlockSpec(memory_space=pltpu.VMEM),
        out_shape=pltpu.VMEM((dirs, 256), F32),
        scratch_shapes=[pltpu.VMEM((1, tok, 256), BF16)],
        compiler_params=pltpu.CompilerParams(vmem_limit_bytes=16 << 20),
        cost_estimate=cost(1),
    )(*act[:parts], rg, mine)
    return pl.pallas_call(
        second_kernel,
        in_specs=[pl.BlockSpec(memory_space=pltpu.SMEM)] + in_vmem(len(act) + 4),
        out_specs=in_vmem(3),
        out_shape=[
            pltpu.HBM((local, 2, dirs // 2, 256), F32),
            pltpu.HBM((local, 2, dirs // 2, 256), F32),
            pltpu.HBM((dirs * 512 // 1024, 8, 128), F32),
        ],
        scratch_shapes=[
            pltpu.VMEM((3, tok, 256), BF16),
            pltpu.VMEM((local, dirs, 256), F32),
            pltpu.VMEM((local, dirs, 256), F32),
        ],
        compiler_params=pltpu.CompilerParams(vmem_limit_bytes=16 << 20),
        cost_estimate=cost(3),
    )(e, *act, rg, mine, other, own)


def scale_kernel(e_ref, lam_ref, keep_ref, got_ref, o_ref, inv):
    e, i = e_ref[0], pl.program_id(0)
    local = keep_ref.shape[0]
    tiles, across = lam_ref.shape[0] // 2, 4

    @pl.when(i == 0)
    def _():
        damp = jnp.sum(jnp.sum(lam_ref[...], axis=0), keepdims=True) * (0.1 / lam_ref.size)
        for j in range(tiles):
            r, c = j // across, j % across
            inv[pl.ds(8 * r, 8), pl.ds(128 * c, 128)] = 1.0 / (lam_ref[2 * j + e] + damp)

    for core in range(2):
        for j in range(local):
            for own in range(2):

                @pl.when((i == core * local + j) & (own == (e == core)))
                def _():
                    src = keep_ref if own else got_ref
                    for side in range(2):
                        at = pl.ds(256 * (core if side == 0 else 1 - core), 256)
                        o_ref[0, :, at] = src[j, side] * inv[:, at]


def scaled_rows(e, lam, keep, got):
    local, _, dirs, _ = keep.shape

    def whole(x):
        return pl.BlockSpec(x.shape, lambda i, e: (0,) * x.ndim)

    return pl.pallas_call(
        scale_kernel,
        grid_spec=pltpu.PrefetchScalarGridSpec(
            num_scalar_prefetch=1,
            grid=(2 * local,),
            in_specs=[whole(lam), whole(keep), whole(got)],
            out_specs=pl.BlockSpec((1, dirs, 512), lambda i, e: (i, 0, 0)),
            scratch_shapes=[pltpu.VMEM((dirs, 512), F32)],
        ),
        out_shape=jax.ShapeDtypeStruct((2 * local, dirs, 512), F32),
        compiler_params=pltpu.CompilerParams(vmem_limit_bytes=8 << 20),
    )(e, lam, keep, got)


def per_device(activations, out_grads, grad_basis, panel_store, owners, token_count):
    local, tok, width = activations.shape
    _, panels, half, pw = panel_store.shape
    n_basis, n_ex = lax.axis_size("basis"), lax.axis_size("ex")
    b, e = lax.axis_index("basis"), lax.axis_index("ex")
    e1 = e.reshape(1).astype(jnp.int32)
    blocks = half // ROWS
    pairs = panels // 2

    slots = laid(panel_store.reshape(pairs, 2 * blocks, ROWS, pw), n_basis)
    arrived = lax.all_to_all(slots.reshape(pairs * n_basis, ROWS, pw), ("ex", "basis"), 0, 0, tiled=True)
    act = turned(activations)
    rg = lax.dot_general(grad_basis, out_grads, (((0,), (2,)), ((), ())), preferred_element_type=F32)
    rg = jnp.transpose(rg, (1, 0, 2)).astype(BF16)
    live = jnp.arange(tok)[None, :] < token_count[:, None]
    rg = jnp.where(live[:, None, :], rg, jnp.zeros((), BF16))
    arrived, act, rg = lax.optimization_barrier((arrived, act, rg))

    owner = owners[2 * e + jnp.where(b < blocks, 0, 1)]
    block = lax.dynamic_index_in_dim(arrived.reshape(2, n_basis, ROWS, pw), owner, 1, keepdims=False)
    spread = jnp.broadcast_to(block[None], (n_basis, 2, ROWS, pw))
    mine = lax.all_to_all(spread, "basis", 0, 0, tiled=True)

    swap = [(0, 1), (1, 0)]
    other = lax.ppermute(mine, "ex", swap)
    keep, send, squares = ex_gradients(e1, act, rg, mine, other)
    got = lax.ppermute(send, "ex", swap)
    both = ("basis", "ex")
    parts = lax.all_to_all(squares, both, 0, 0, tiled=True)
    lam = jnp.sum(parts, axis=0, keepdims=True) * (1.0 / (local * n_basis * n_ex))
    lam = lax.all_to_all(jnp.broadcast_to(lam, parts.shape), both, 0, 0, tiled=True)
    return scaled_rows(e1, lam, keep, got)


def solution(mesh):
    return jax.shard_map(
        per_device,
        mesh=mesh,
        in_specs=(
            P(("basis", "ex"), None, None),
            P(("basis", "ex"), None, None),
            P(),
            P("basis", None, "ex", None),
            P(),
            P(("basis", "ex")),
        ),
        out_specs=P("basis", "ex", None),
        check_vma=False,
    )
```

```python
import functools

import jax
import jax.numpy as jnp
from jax import lax
from jax.experimental import pallas as pl
from jax.experimental.pallas import tpu as pltpu
from jax.sharding import PartitionSpec as P

ROWS = 24
TT = 256
GT = 768
F32 = jnp.float32
BF16 = jnp.bfloat16


def in_vmem(n):
    return [pl.BlockSpec(memory_space=pltpu.VMEM)] * n


def lay_kernel(cuts, owners_ref, x_ref, o_ref, shared_ref, held, sems):
    pairs, blocks = held.shape[:2]
    step = blocks // cuts
    me = lax.axis_index("basis")
    takes, gives = [], []
    for p in range(pairs):
        second = (owners_ref[2 * p] != me) & (owners_ref[2 * p + 1] == me)
        panel = 2 * p + jnp.where(second, 1, 0)
        for i in range(cuts):
            at = pl.ds(i * step, step)
            k = p * cuts + i
            takes.append(pltpu.make_async_copy(x_ref.at[panel, at], held.at[p, at], sems.at[0, k]))
            gives.append(pltpu.make_async_copy(held.at[p, at], o_ref.at[p, at], sems.at[1, k]))
    for c in takes:
        c.start()
    shared = [jnp.where(owners_ref[2 * p] == owners_ref[2 * p + 1], 1, 0) for p in range(pairs)]
    shared_ref[0] = sum(shared)
    for c, d in zip(takes, gives):
        c.wait()
        d.start()
    for d in gives:
        d.wait()


def laid(owners, slots, n_basis):
    panels, blocks, rows, width = slots.shape
    pairs, cuts = panels // 2, 3
    return pl.pallas_call(
        functools.partial(lay_kernel, cuts),
        in_specs=[pl.BlockSpec(memory_space=pltpu.SMEM), pl.BlockSpec(memory_space=pl.ANY)],
        out_specs=[pl.BlockSpec(memory_space=pl.ANY), pl.BlockSpec(memory_space=pltpu.SMEM)],
        out_shape=[
            pltpu.HBM((pairs, n_basis, rows, width), slots.dtype),
            jax.ShapeDtypeStruct((1,), jnp.int32),
        ],
        scratch_shapes=[
            pltpu.VMEM((pairs, blocks, rows, width), slots.dtype),
            pltpu.SemaphoreType.DMA((2, pairs * cuts)),
        ],
        compiler_params=pltpu.CompilerParams(vmem_limit_bytes=4 << 20),
    )(owners, pltpu.with_memory_space_constraint(slots, pltpu.HBM))


def pick_kernel(owners_ref, x_ref, second_ref, o_ref, block, sems):
    rows = x_ref.shape[2]
    first = 2 * lax.axis_index("ex")
    owner0, owner1 = owners_ref[first], owners_ref[first + 1]

    def fetches(second):
        src = second_ref if second else x_ref.at[:, owner1]
        out = []
        for h in range(2):
            at = pl.ds(h * rows, rows)
            out.append(pltpu.make_async_copy(x_ref.at[h, owner0], block.at[0, at], sems.at[h]))
            out.append(pltpu.make_async_copy(src.at[h], block.at[1, at], sems.at[2 + h]))
        return out

    for second in range(2):

        @pl.when((owner0 == owner1) == bool(second))
        def _():
            for c in fetches(second):
                c.start()
            for c in fetches(second):
                c.wait()

    for j in range(o_ref.shape[0]):
        o_ref[j] = block[...]


def picked(owners, arrived, second):
    _, n_basis, rows, width = arrived.shape
    return pl.pallas_call(
        pick_kernel,
        in_specs=[pl.BlockSpec(memory_space=pltpu.SMEM)] + [pl.BlockSpec(memory_space=pl.ANY)] * 2,
        out_specs=pl.BlockSpec(memory_space=pltpu.VMEM),
        out_shape=pltpu.VMEM((n_basis, 2, 2 * rows, width), arrived.dtype),
        scratch_shapes=[pltpu.VMEM((2, 2 * rows, width), arrived.dtype), pltpu.SemaphoreType.DMA((4,))],
        compiler_params=pltpu.CompilerParams(vmem_limit_bytes=1 << 20),
    )(owners, arrived, second)


def rot_grad_kernel(count_ref, basis_ref, x_ref, o_ref, turned_basis):
    n, t = pl.program_id(0), pl.program_id(1)
    step = o_ref.shape[2]

    @pl.when((n == 0) & (t == 0))
    def _():
        turned_basis[...] = basis_ref[...].T

    rot = jnp.dot(turned_basis[...], x_ref[0], preferred_element_type=F32).astype(BF16)
    live = t * step + lax.broadcasted_iota(jnp.int32, rot.shape, 1) < count_ref[n]
    o_ref[0] = jnp.where(live, rot, jnp.zeros_like(rot))


def rotated_grads(token_count, grad_basis, out_grads):
    local, tok, width = out_grads.shape
    dirs = grad_basis.shape[1]
    x = pltpu.with_memory_space_constraint(jnp.swapaxes(out_grads, 1, 2), pltpu.HBM)
    return pl.pallas_call(
        rot_grad_kernel,
        grid_spec=pltpu.PrefetchScalarGridSpec(
            num_scalar_prefetch=1,
            grid=(local, tok // GT),
            in_specs=[
                pl.BlockSpec((width, dirs), lambda n, t, count: (0, 0)),
                pl.BlockSpec((1, width, GT), lambda n, t, count: (n, 0, t)),
            ],
            out_specs=pl.BlockSpec((1, dirs, GT), lambda n, t, count: (n, 0, t)),
            scratch_shapes=[pltpu.VMEM((dirs, width), BF16)],
        ),
        out_shape=jax.ShapeDtypeStruct((local, dirs, tok), BF16),
        compiler_params=pltpu.CompilerParams(vmem_limit_bytes=28 << 20),
        cost_estimate=pl.CostEstimate(
            flops=2 * local * tok * width * dirs, transcendentals=0, bytes_accessed=2 * local * tok * width
        ),
    )(token_count, grad_basis, x)


def turn_kernel(x_ref, *o_refs):
    parts = x_ref.shape[2] // TT
    for i, o_ref in enumerate(o_refs):

        @pl.when(pl.program_id(0) == i // parts)
        def _():
            x = x_ref[0, :, pl.ds(i % parts * TT, TT)].reshape(2, -1, ROWS, TT)
            o_ref[...] = jnp.swapaxes(x, 0, 1).reshape(-1, TT).T


def turned(activations):
    local, tok, width = activations.shape
    x = pltpu.with_memory_space_constraint(jnp.swapaxes(activations, 1, 2), pltpu.HBM)
    count = local * tok // TT
    return pl.pallas_call(
        turn_kernel,
        grid=(local,),
        in_specs=[pl.BlockSpec((1, width, tok), lambda n: (n, 0, 0))],
        out_specs=[pl.BlockSpec((TT, width), lambda n: (0, 0))] * count,
        out_shape=[pltpu.HBM((TT, width), BF16)] * count,
        compiler_params=pltpu.CompilerParams(vmem_limit_bytes=40 << 20),
        cost_estimate=pl.CostEstimate(flops=0, transcendentals=0, bytes_accessed=4 * local * tok * width),
    )(x)


def pair_of_panels(ref, width):
    senders = width // ref.shape[2]
    return jnp.concatenate([ref[pl.ds(0, senders), k].reshape(width, 128) for k in range(2)], axis=1)


def rotate(act_refs, pair, rot, slot):
    for t, act_ref in enumerate(act_refs):
        rot[slot, pl.ds(t * TT, TT)] = jnp.dot(act_ref[...], pair, preferred_element_type=F32).astype(BF16)


def first_kernel(*refs):
    *act_refs, rg_ref, basis_ref, ex_ref, rot = refs
    rotate(act_refs, pair_of_panels(basis_ref, act_refs[0].shape[1]), rot, 0)
    ex_ref[...] = jnp.dot(rg_ref[0], rot[0], preferred_element_type=F32)


def second_kernel(*refs):
    *act_refs, rg_ref, mine_ref, other_ref, own0_ref, keep_ref, send_ref, sq_ref, rot, own_ref, ex_ref = refs
    e = lax.axis_index("ex")
    local, dirs, cols = own_ref.shape
    mid = dirs // 2
    parts, width = len(act_refs) // local, act_refs[0].shape[1]
    rotate(act_refs[parts:], pair_of_panels(mine_ref, width), rot, 0)
    pair = pair_of_panels(other_ref, width)
    rotate(act_refs[:parts], pair, rot, 1)
    rotate(act_refs[parts:], pair, rot, 2)
    own_ref[0] = own0_ref[...]
    own_ref[1] = jnp.dot(rg_ref[1], rot[0], preferred_element_type=F32)
    for n in range(local):
        ex_ref[n] = jnp.dot(rg_ref[n], rot[1 + n], preferred_element_type=F32)
    here, there = (pl.ds(pl.multiple_of(x * mid, 8), mid) for x in (e, 1 - e))
    for n in range(local):
        for side, src in enumerate((own_ref, ex_ref)):
            keep_ref[n, side] = src[n, here, :]
            send_ref[n, side] = src[n, there, :]
    for side, src in enumerate((own_ref, ex_ref)):
        pair = e if side == 0 else 1 - e
        for h in range(2):
            for r in range(mid // 8):
                for c in range(cols // 128):
                    at = (pl.ds(h * mid + 8 * r, 8), pl.ds(128 * c, 128))
                    tile = src[0, at[0], at[1]] * src[0, at[0], at[1]]
                    for n in range(1, local):
                        tile += src[n, at[0], at[1]] * src[n, at[0], at[1]]
                    sq_ref[2 * (2 * (cols // 128) * r + (cols // 128) * pair + c) + h] = tile


def ex_gradients(act, rg, mine, other):
    local, dirs, tok = rg.shape
    width = act[0].shape[1]
    parts = len(act) // local

    def cost(count):
        return pl.CostEstimate(
            flops=2 * count * tok * width * 256, transcendentals=0, bytes_accessed=2 * count * tok * width
        )

    own = pl.pallas_call(
        first_kernel,
        in_specs=in_vmem(parts + 2),
        out_specs=pl.BlockSpec(memory_space=pltpu.VMEM),
        out_shape=pltpu.VMEM((dirs, 256), F32),
        scratch_shapes=[pltpu.VMEM((1, tok, 256), BF16)],
        compiler_params=pltpu.CompilerParams(vmem_limit_bytes=16 << 20),
        cost_estimate=cost(1),
    )(*act[:parts], rg, mine)
    return pl.pallas_call(
        second_kernel,
        in_specs=in_vmem(len(act) + 4),
        out_specs=in_vmem(3),
        out_shape=[
            pltpu.HBM((local, 2, dirs // 2, 256), F32),
            pltpu.HBM((local, 2, dirs // 2, 256), F32),
            pltpu.HBM((dirs * 512 // 1024, 8, 128), F32),
        ],
        scratch_shapes=[
            pltpu.VMEM((3, tok, 256), BF16),
            pltpu.VMEM((local, dirs, 256), F32),
            pltpu.VMEM((local, dirs, 256), F32),
        ],
        compiler_params=pltpu.CompilerParams(vmem_limit_bytes=16 << 20),
        cost_estimate=cost(3),
    )(*act, rg, mine, other, own)


def scale_kernel(lam_ref, keep_ref, got_ref, o_ref, inv):
    e, i = lax.axis_index("ex"), pl.program_id(0)
    local = keep_ref.shape[0]
    tiles, across = lam_ref.shape[0] // 2, 4

    @pl.when(i == 0)
    def _():
        damp = jnp.sum(jnp.sum(lam_ref[...], axis=0), keepdims=True) * (0.1 / lam_ref.size)
        for j in range(tiles):
            r, c = j // across, j % across
            inv[pl.ds(8 * r, 8), pl.ds(128 * c, 128)] = 1.0 / (lam_ref[2 * j + e] + damp)

    for core in range(2):
        for j in range(local):
            for own in range(2):

                @pl.when((i == core * local + j) & (own == (e == core)))
                def _():
                    src = keep_ref if own else got_ref
                    for side in range(2):
                        at = pl.ds(256 * (core if side == 0 else 1 - core), 256)
                        o_ref[0, :, at] = src[j, side] * inv[:, at]


def scaled_rows(lam, keep, got):
    local, _, dirs, _ = keep.shape

    def whole(x):
        return pl.BlockSpec(x.shape, lambda i: (0,) * x.ndim)

    return pl.pallas_call(
        scale_kernel,
        grid=(2 * local,),
        in_specs=[whole(lam), whole(keep), whole(got)],
        out_specs=pl.BlockSpec((1, dirs, 512), lambda i: (i, 0, 0)),
        scratch_shapes=[pltpu.VMEM((dirs, 512), F32)],
        out_shape=jax.ShapeDtypeStruct((2 * local, dirs, 512), F32),
        compiler_params=pltpu.CompilerParams(vmem_limit_bytes=8 << 20),
    )(lam, keep, got)


def per_device(activations, out_grads, grad_basis, panel_store, owners, token_count):
    local, tok, width = activations.shape
    _, panels, half, pw = panel_store.shape
    n_basis, n_ex = lax.axis_size("basis"), lax.axis_size("ex")
    blocks = half // ROWS

    slots = panel_store.reshape(panels, blocks, ROWS, pw)
    sent, shared = laid(owners, slots, n_basis)

    def to_chips(x):
        got = lax.all_to_all(x.reshape(-1, ROWS, pw), ("ex", "basis"), 0, 0, tiled=True)
        return got.reshape(2, n_basis, ROWS, pw)

    arrived = to_chips(sent)
    act = turned(activations)
    rg = rotated_grads(token_count, grad_basis, out_grads)
    arrived, slots, act, rg = lax.optimization_barrier((arrived, slots, act, rg))

    def second_panels(slots):
        second = to_chips(jnp.pad(slots[1::2], ((0, 0), (0, n_basis - blocks), (0, 0), (0, 0))))
        owner = owners[2 * lax.axis_index("ex") + 1]
        return lax.dynamic_index_in_dim(second, owner, 1, keepdims=False)

    second = lax.cond(
        shared[0] > 0, second_panels, lambda slots: jnp.zeros((2, ROWS, pw), slots.dtype), slots
    )
    mine = lax.all_to_all(picked(owners, arrived, second), "basis", 0, 0, tiled=True)

    swap = [(0, 1), (1, 0)]
    other = lax.ppermute(mine, "ex", swap)
    keep, send, squares = ex_gradients(act, rg, mine, other)
    got = lax.ppermute(send, "ex", swap)
    both = ("basis", "ex")
    parts = lax.all_to_all(squares, both, 0, 0, tiled=True)
    lam = jnp.sum(parts, axis=0, keepdims=True) * (1.0 / (local * n_basis * n_ex))
    lam = lax.all_to_all(jnp.broadcast_to(lam, parts.shape), both, 0, 0, tiled=True)
    return scaled_rows(lam, keep, got)


def solution(mesh):
    return jax.shard_map(
        per_device,
        mesh=mesh,
        in_specs=(
            P(("basis", "ex"), None, None),
            P(("basis", "ex"), None, None),
            P(),
            P("basis", None, "ex", None),
            P(),
            P(("basis", "ex")),
        ),
        out_specs=P("basis", "ex", None),
        check_vma=False,
    )
```

```python
import functools

import jax
import jax.numpy as jnp
from jax import lax
from jax.experimental import pallas as pl
from jax.experimental.pallas import tpu as pltpu
from jax.sharding import PartitionSpec as P

ROWS = 24
TT = 256
GT = 768
F32 = jnp.float32
BF16 = jnp.bfloat16


def in_vmem(n):
    return [pl.BlockSpec(memory_space=pltpu.VMEM)] * n


def lay_kernel(cuts, owners_ref, x_ref, o_ref, held, sems):
    pairs, blocks = held.shape[:2]
    step = blocks // cuts
    me = lax.axis_index("basis")
    takes, gives = [], []
    for p in range(pairs):
        second = (owners_ref[2 * p] != me) & (owners_ref[2 * p + 1] == me)
        panel = 2 * p + jnp.where(second, 1, 0)
        for i in range(cuts):
            at = pl.ds(i * step, step)
            k = p * cuts + i
            takes.append(pltpu.make_async_copy(x_ref.at[panel, at], held.at[p, at], sems.at[0, k]))
            gives.append(pltpu.make_async_copy(held.at[p, at], o_ref.at[p, at], sems.at[1, k]))
    for c in takes:
        c.start()
    for c, d in zip(takes, gives):
        c.wait()
        d.start()
    for d in gives:
        d.wait()


def laid(owners, slots, n_basis):
    panels, blocks, rows, width = slots.shape
    pairs, cuts = panels // 2, 3
    return pl.pallas_call(
        functools.partial(lay_kernel, cuts),
        in_specs=[pl.BlockSpec(memory_space=pltpu.SMEM), pl.BlockSpec(memory_space=pl.ANY)],
        out_specs=pl.BlockSpec(memory_space=pl.ANY),
        out_shape=pltpu.HBM((pairs, n_basis, rows, width), slots.dtype),
        scratch_shapes=[
            pltpu.VMEM((pairs, blocks, rows, width), slots.dtype),
            pltpu.SemaphoreType.DMA((2, pairs * cuts)),
        ],
        compiler_params=pltpu.CompilerParams(vmem_limit_bytes=4 << 20),
    )(owners, pltpu.with_memory_space_constraint(slots, pltpu.HBM))


def pick_kernel(owners_ref, x_ref, second_ref, o_ref, block, sems):
    rows = x_ref.shape[2]
    first = 2 * lax.axis_index("ex")
    owner0, owner1 = owners_ref[first], owners_ref[first + 1]

    def fetches(second):
        src = second_ref if second else x_ref.at[:, owner1]
        out = []
        for h in range(2):
            at = pl.ds(h * rows, rows)
            out.append(pltpu.make_async_copy(x_ref.at[h, owner0], block.at[0, at], sems.at[h]))
            out.append(pltpu.make_async_copy(src.at[h], block.at[1, at], sems.at[2 + h]))
        return out

    for second in range(2):

        @pl.when((owner0 == owner1) == bool(second))
        def _():
            for c in fetches(second):
                c.start()
            for c in fetches(second):
                c.wait()

    for j in range(o_ref.shape[0]):
        o_ref[j] = block[...]


def picked(owners, arrived, second):
    _, n_basis, rows, width = arrived.shape
    return pl.pallas_call(
        pick_kernel,
        in_specs=[pl.BlockSpec(memory_space=pltpu.SMEM)] + [pl.BlockSpec(memory_space=pl.ANY)] * 2,
        out_specs=pl.BlockSpec(memory_space=pltpu.VMEM),
        out_shape=pltpu.VMEM((n_basis, 2, 2 * rows, width), arrived.dtype),
        scratch_shapes=[pltpu.VMEM((2, 2 * rows, width), arrived.dtype), pltpu.SemaphoreType.DMA((4,))],
        compiler_params=pltpu.CompilerParams(vmem_limit_bytes=1 << 20),
    )(owners, arrived, second)


def rot_grad_kernel(count_ref, basis_ref, x_ref, o_ref, turned_basis):
    n, t = pl.program_id(0), pl.program_id(1)
    step = o_ref.shape[2]

    @pl.when((n == 0) & (t == 0))
    def _():
        turned_basis[...] = basis_ref[...].T

    rot = jnp.dot(turned_basis[...], x_ref[0], preferred_element_type=F32).astype(BF16)
    live = t * step + lax.broadcasted_iota(jnp.int32, rot.shape, 1) < count_ref[n]
    o_ref[0] = jnp.where(live, rot, jnp.zeros_like(rot))


def rotated_grads(token_count, grad_basis, out_grads):
    local, tok, width = out_grads.shape
    dirs = grad_basis.shape[1]
    x = pltpu.with_memory_space_constraint(jnp.swapaxes(out_grads, 1, 2), pltpu.HBM)
    return pl.pallas_call(
        rot_grad_kernel,
        grid_spec=pltpu.PrefetchScalarGridSpec(
            num_scalar_prefetch=1,
            grid=(local, tok // GT),
            in_specs=[
                pl.BlockSpec((width, dirs), lambda n, t, count: (0, 0)),
                pl.BlockSpec((1, width, GT), lambda n, t, count: (n, 0, t)),
            ],
            out_specs=pl.BlockSpec((1, dirs, GT), lambda n, t, count: (n, 0, t)),
            scratch_shapes=[pltpu.VMEM((dirs, width), BF16)],
        ),
        out_shape=jax.ShapeDtypeStruct((local, dirs, tok), BF16),
        compiler_params=pltpu.CompilerParams(vmem_limit_bytes=28 << 20),
        cost_estimate=pl.CostEstimate(
            flops=2 * local * tok * width * dirs, transcendentals=0, bytes_accessed=2 * local * tok * width
        ),
    )(token_count, grad_basis, x)


def take_kernel(owners_ref, x_ref, o_ref, shared_ref, held, sems):
    cuts = sems.shape[1]
    step = o_ref.shape[0] // cuts
    takes, gives = [], []
    for i in range(cuts):
        at = pl.ds(i * step, step)
        takes.append(pltpu.make_async_copy(x_ref.at[0, at], held.at[at], sems.at[0, i]))
        gives.append(pltpu.make_async_copy(held.at[at], o_ref.at[at], sems.at[1, i]))
    for c in takes:
        c.start()
    shared = [owners_ref[p] == owners_ref[p + 1] for p in range(0, owners_ref.shape[0], 2)]
    shared_ref[0] = sum(jnp.where(same, 1, 0) for same in shared)
    for c, d in zip(takes, gives):
        c.wait()
        d.start()
    for d in gives:
        d.wait()


def first_example(owners, activations):
    _, tok, width = activations.shape
    x = pltpu.with_memory_space_constraint(jnp.swapaxes(activations, 1, 2), pltpu.HBM)
    return pl.pallas_call(
        take_kernel,
        in_specs=[pl.BlockSpec(memory_space=pltpu.SMEM), pl.BlockSpec(memory_space=pl.ANY)],
        out_specs=[pl.BlockSpec(memory_space=pl.ANY), pl.BlockSpec(memory_space=pltpu.SMEM)],
        out_shape=[pltpu.HBM((width, tok), BF16), jax.ShapeDtypeStruct((1,), jnp.int32)],
        scratch_shapes=[pltpu.VMEM((width, tok), BF16), pltpu.SemaphoreType.DMA((2, 6))],
        compiler_params=pltpu.CompilerParams(vmem_limit_bytes=12 << 20),
        cost_estimate=pl.CostEstimate(flops=0, transcendentals=0, bytes_accessed=4 * tok * width),
    )(owners, x)


def pair_of_panels(ref, width):
    senders = width // ref.shape[2]
    panels = []
    for k in range(2):
        x = ref[pl.ds(0, senders), k].reshape(senders, 2, ROWS, 128)
        panels.append(jnp.swapaxes(x, 0, 1).reshape(width, 128))
    return jnp.concatenate(panels, axis=1).T


def rotate(act_ref, pair_ref, rot, slot):
    for t in range(0, act_ref.shape[1], TT):
        at = pl.ds(t, TT)
        rot[slot, :, at] = jnp.dot(pair_ref[...], act_ref[:, at], preferred_element_type=F32).astype(BF16)


def gradients(rg, rot):
    return lax.dot_general(rg, rot, (((1,), (1,)), ((), ())), preferred_element_type=F32)


def first_kernel(act_ref, rg_ref, basis_ref, ex_ref, pair_ref, rot):
    pair_ref[...] = pair_of_panels(basis_ref, act_ref.shape[0])
    rotate(act_ref, pair_ref, rot, 0)
    ex_ref[...] = gradients(rg_ref[0], rot[0])


def second_kernel(*refs):
    act0_ref, act1_ref, rg_ref, mine_ref, other_ref, own0_ref, keep_ref, send_ref, sq_ref, rot, own_ref, ex_ref, pair_ref = refs
    e = lax.axis_index("ex")
    local, dirs, cols = own_ref.shape
    mid = dirs // 2
    rotate(act1_ref, mine_ref, rot, 0)
    pair_ref[...] = pair_of_panels(other_ref, act0_ref.shape[0])
    rotate(act0_ref, pair_ref, rot, 1)
    rotate(act1_ref, pair_ref, rot, 2)
    own_ref[0] = own0_ref[...]
    own_ref[1] = gradients(rg_ref[1], rot[0])
    for n in range(local):
        ex_ref[n] = gradients(rg_ref[n], rot[1 + n])
    here, there = (pl.ds(pl.multiple_of(x * mid, 8), mid) for x in (e, 1 - e))
    for n in range(local):
        for side, src in enumerate((own_ref, ex_ref)):
            keep_ref[n, side] = src[n, here, :]
            send_ref[n, side] = src[n, there, :]
    for side, src in enumerate((own_ref, ex_ref)):
        pair = e if side == 0 else 1 - e
        for h in range(2):
            for r in range(mid // 8):
                for c in range(cols // 128):
                    at = (pl.ds(h * mid + 8 * r, 8), pl.ds(128 * c, 128))
                    tile = src[0, at[0], at[1]] * src[0, at[0], at[1]]
                    for n in range(1, local):
                        tile += src[n, at[0], at[1]] * src[n, at[0], at[1]]
                    sq_ref[2 * (2 * (cols // 128) * r + (cols // 128) * pair + c) + h] = tile


def ex_gradients(act, rg, mine, other):
    local, dirs, tok = rg.shape
    width = act[0].shape[0]

    def cost(count):
        return pl.CostEstimate(
            flops=2 * count * tok * width * 256, transcendentals=0, bytes_accessed=2 * count * tok * width
        )

    own, pair = pl.pallas_call(
        first_kernel,
        in_specs=in_vmem(3),
        out_specs=in_vmem(2),
        out_shape=[pltpu.VMEM((dirs, 256), F32), pltpu.VMEM((256, width), BF16)],
        scratch_shapes=[pltpu.VMEM((1, 256, tok), BF16)],
        compiler_params=pltpu.CompilerParams(vmem_limit_bytes=16 << 20),
        cost_estimate=cost(1),
    )(act[0], rg, mine)
    return pl.pallas_call(
        second_kernel,
        in_specs=in_vmem(6),
        out_specs=in_vmem(3),
        out_shape=[
            pltpu.HBM((local, 2, dirs // 2, 256), F32),
            pltpu.HBM((local, 2, dirs // 2, 256), F32),
            pltpu.HBM((dirs * 512 // 1024, 8, 128), F32),
        ],
        scratch_shapes=[
            pltpu.VMEM((3, 256, tok), BF16),
            pltpu.VMEM((local, dirs, 256), F32),
            pltpu.VMEM((local, dirs, 256), F32),
            pltpu.VMEM((256, width), BF16),
        ],
        compiler_params=pltpu.CompilerParams(vmem_limit_bytes=16 << 20),
        cost_estimate=cost(3),
    )(*act, rg, pair, other, own)


def scale_kernel(lam_ref, keep_ref, got_ref, o_ref, inv, held, sem):
    e, i = lax.axis_index("ex"), pl.program_id(0)
    local = keep_ref.shape[0]
    tiles, across = lam_ref.shape[0] // 2, 4

    @pl.when(i == 0)
    def _():
        fetch = pltpu.make_async_copy(keep_ref, held, sem)
        fetch.start()
        damp = jnp.sum(jnp.sum(lam_ref[...], axis=0), keepdims=True) * (0.1 / lam_ref.size)
        for j in range(tiles):
            r, c = j // across, j % across
            inv[pl.ds(8 * r, 8), pl.ds(128 * c, 128)] = 1.0 / (lam_ref[2 * j + e] + damp)
        fetch.wait()

    for core in range(2):
        for j in range(local):
            for own in range(2):

                @pl.when((i == core * local + j) & (own == (e == core)))
                def _():
                    src = held if own else got_ref
                    for side in range(2):
                        at = pl.ds(256 * (core if side == 0 else 1 - core), 256)
                        o_ref[0, :, at] = src[j, side] * inv[:, at]


def scaled_rows(lam, keep, got):
    local, _, dirs, _ = keep.shape

    def whole(x):
        return pl.BlockSpec(x.shape, lambda i: (0,) * x.ndim)

    return pl.pallas_call(
        scale_kernel,
        grid=(2 * local,),
        in_specs=[whole(lam), pl.BlockSpec(memory_space=pl.ANY), whole(got)],
        out_specs=pl.BlockSpec((1, dirs, 512), lambda i: (i, 0, 0)),
        scratch_shapes=[pltpu.VMEM((dirs, 512), F32), pltpu.VMEM(keep.shape, F32), pltpu.SemaphoreType.DMA],
        out_shape=jax.ShapeDtypeStruct((2 * local, dirs, 512), F32),
        compiler_params=pltpu.CompilerParams(vmem_limit_bytes=8 << 20),
    )(lam, pltpu.with_memory_space_constraint(keep, pltpu.HBM), got)


def per_device(activations, out_grads, grad_basis, panel_store, owners, token_count):
    local, tok, width = activations.shape
    _, panels, half, pw = panel_store.shape
    n_basis, n_ex = lax.axis_size("basis"), lax.axis_size("ex")
    blocks = half // ROWS

    slots = panel_store.reshape(panels, blocks, ROWS, pw)
    sent = laid(owners, slots, n_basis)

    def to_chips(x):
        got = lax.all_to_all(x.reshape(-1, ROWS, pw), ("ex", "basis"), 0, 0, tiled=True)
        return got.reshape(2, n_basis, ROWS, pw)

    arrived = to_chips(sent)
    act0, shared = first_example(owners, activations)
    rg = rotated_grads(token_count, grad_basis, out_grads)
    arrived, slots, act0, rg = lax.optimization_barrier((arrived, slots, act0, rg))
    act = [act0, activations[1].T]

    def second_panels(slots):
        second = to_chips(jnp.pad(slots[1::2], ((0, 0), (0, n_basis - blocks), (0, 0), (0, 0))))
        owner = owners[2 * lax.axis_index("ex") + 1]
        return lax.dynamic_index_in_dim(second, owner, 1, keepdims=False)

    second = lax.cond(
        shared[0] > 0, second_panels, lambda slots: jnp.zeros((2, ROWS, pw), slots.dtype), slots
    )
    mine = lax.all_to_all(picked(owners, arrived, second), "basis", 0, 0, tiled=True)

    swap = [(0, 1), (1, 0)]
    other = lax.ppermute(mine, "ex", swap)
    keep, send, squares = ex_gradients(act, rg, mine, other)
    got = lax.ppermute(send, "ex", swap)
    both = ("basis", "ex")
    parts = lax.all_to_all(squares, both, 0, 0, tiled=True)
    lam = jnp.sum(parts, axis=0, keepdims=True) * (1.0 / (local * n_basis * n_ex))
    lam = lax.all_to_all(jnp.broadcast_to(lam, parts.shape), both, 0, 0, tiled=True)
    return scaled_rows(lam, keep, got)


def solution(mesh):
    return jax.shard_map(
        per_device,
        mesh=mesh,
        in_specs=(
            P(("basis", "ex"), None, None),
            P(("basis", "ex"), None, None),
            P(),
            P("basis", None, "ex", None),
            P(),
            P(("basis", "ex")),
        ),
        out_specs=P("basis", "ex", None),
        check_vma=False,
    )
```

```python
import functools

import jax
import jax.numpy as jnp
from jax import lax
from jax.experimental import pallas as pl
from jax.experimental.pallas import tpu as pltpu
from jax.sharding import PartitionSpec as P

ROWS = 24
TT = 256
F32 = jnp.float32
BF16 = jnp.bfloat16


def in_vmem(n):
    return [pl.BlockSpec(memory_space=pltpu.VMEM)] * n


def lay_kernel(cuts, owners_ref, x_ref, o_ref, held, sems):
    pairs, blocks = held.shape[:2]
    step = blocks // cuts
    me = lax.axis_index("basis")
    takes, gives = [], []
    for p in range(pairs):
        second = (owners_ref[2 * p] != me) & (owners_ref[2 * p + 1] == me)
        panel = 2 * p + jnp.where(second, 1, 0)
        for i in range(cuts):
            at = pl.ds(i * step, step)
            k = p * cuts + i
            takes.append(pltpu.make_async_copy(x_ref.at[panel, at], held.at[p, at], sems.at[0, k]))
            gives.append(pltpu.make_async_copy(held.at[p, at], o_ref.at[p, at], sems.at[1, k]))
    for c in takes:
        c.start()
    for c, d in zip(takes, gives):
        c.wait()
        d.start()
    for d in gives:
        d.wait()


def laid(owners, slots, n_basis):
    panels, blocks, rows, width = slots.shape
    pairs, cuts = panels // 2, 3
    return pl.pallas_call(
        functools.partial(lay_kernel, cuts),
        in_specs=[pl.BlockSpec(memory_space=pltpu.SMEM), pl.BlockSpec(memory_space=pl.ANY)],
        out_specs=pl.BlockSpec(memory_space=pl.ANY),
        out_shape=pltpu.HBM((pairs, n_basis, rows, width), slots.dtype),
        scratch_shapes=[
            pltpu.VMEM((pairs, blocks, rows, width), slots.dtype),
            pltpu.SemaphoreType.DMA((2, pairs * cuts)),
        ],
        compiler_params=pltpu.CompilerParams(vmem_limit_bytes=4 << 20),
    )(owners, pltpu.with_memory_space_constraint(slots, pltpu.HBM))


def pick_kernel(owners_ref, x_ref, second_ref, o_ref, block, sems):
    rows = x_ref.shape[2]
    first = 2 * lax.axis_index("ex")
    owner0, owner1 = owners_ref[first], owners_ref[first + 1]

    def fetches(second):
        src = second_ref if second else x_ref.at[:, owner1]
        out = []
        for h in range(2):
            at = pl.ds(h * rows, rows)
            out.append(pltpu.make_async_copy(x_ref.at[h, owner0], block.at[0, at], sems.at[h]))
            out.append(pltpu.make_async_copy(src.at[h], block.at[1, at], sems.at[2 + h]))
        return out

    for second in range(2):

        @pl.when((owner0 == owner1) == bool(second))
        def _():
            for c in fetches(second):
                c.start()
            for c in fetches(second):
                c.wait()

    for j in range(o_ref.shape[0]):
        o_ref[j] = block[...]


def picked(owners, arrived, second):
    _, n_basis, rows, width = arrived.shape
    return pl.pallas_call(
        pick_kernel,
        in_specs=[pl.BlockSpec(memory_space=pltpu.SMEM)] + [pl.BlockSpec(memory_space=pl.ANY)] * 2,
        out_specs=pl.BlockSpec(memory_space=pltpu.VMEM),
        out_shape=pltpu.VMEM((n_basis, 2, 2 * rows, width), arrived.dtype),
        scratch_shapes=[pltpu.VMEM((2, 2 * rows, width), arrived.dtype), pltpu.SemaphoreType.DMA((4,))],
        compiler_params=pltpu.CompilerParams(vmem_limit_bytes=1 << 20),
    )(owners, arrived, second)


def early_kernel(owners_ref, count_ref, basis_ref, grads_ref, act_ref, rg_ref, act0_ref, shared_ref, grads, held, sems):
    local = grads.shape[0]
    reads = [pltpu.make_async_copy(grads_ref.at[n], grads.at[n], sems.at[n]) for n in range(local)]
    take = pltpu.make_async_copy(act_ref.at[0], held, sems.at[local])
    give = pltpu.make_async_copy(held, act0_ref, sems.at[local + 1])
    for c in (reads[0], take, *reads[1:]):
        c.start()
    shared = [owners_ref[p] == owners_ref[p + 1] for p in range(0, owners_ref.shape[0], 2)]
    shared_ref[0] = sum(jnp.where(same, 1, 0) for same in shared)
    turned = basis_ref[...].T
    for n in range(local):
        reads[n].wait()
        if n == 0:
            take.wait()
            give.start()
        rot = jnp.dot(turned, grads[n], preferred_element_type=F32).astype(BF16)
        live = lax.broadcasted_iota(jnp.int32, rot.shape, 1) < count_ref[n]
        rg_ref[n] = jnp.where(live, rot, jnp.zeros_like(rot))
    give.wait()


def early(owners, token_count, grad_basis, out_grads, activations):
    local, tok, width = out_grads.shape
    dirs = grad_basis.shape[1]
    grads, act = (
        pltpu.with_memory_space_constraint(jnp.swapaxes(x, 1, 2), pltpu.HBM) for x in (out_grads, activations)
    )
    smem, hbm = pl.BlockSpec(memory_space=pltpu.SMEM), pl.BlockSpec(memory_space=pl.ANY)
    return pl.pallas_call(
        early_kernel,
        in_specs=[smem, smem, *in_vmem(1), hbm, hbm],
        out_specs=[*in_vmem(1), hbm, smem],
        out_shape=[
            jax.ShapeDtypeStruct((local, dirs, tok), BF16),
            pltpu.HBM((width, tok), BF16),
            jax.ShapeDtypeStruct((1,), jnp.int32),
        ],
        scratch_shapes=[
            pltpu.VMEM((local, width, tok), BF16),
            pltpu.VMEM((width, tok), BF16),
            pltpu.SemaphoreType.DMA((local + 2,)),
        ],
        compiler_params=pltpu.CompilerParams(vmem_limit_bytes=28 << 20),
        cost_estimate=pl.CostEstimate(
            flops=2 * local * tok * width * dirs, transcendentals=0, bytes_accessed=4 * local * tok * width
        ),
    )(owners, token_count, grad_basis, grads, act)


def pair_of_panels(ref, width):
    senders = width // ref.shape[2]
    panels = []
    for k in range(2):
        x = ref[pl.ds(0, senders), k].reshape(senders, 2, ROWS, 128)
        panels.append(jnp.swapaxes(x, 0, 1).reshape(width, 128))
    return jnp.concatenate(panels, axis=1).T


def rotate(act_ref, pair_ref, rot, slot):
    for t in range(0, act_ref.shape[1], TT):
        at = pl.ds(t, TT)
        rot[slot, :, at] = jnp.dot(pair_ref[...], act_ref[:, at], preferred_element_type=F32).astype(BF16)


def gradients(rg, rot):
    return lax.dot_general(rg, rot, (((1,), (1,)), ((), ())), preferred_element_type=F32)


def first_kernel(act_ref, rg_ref, basis_ref, ex_ref, pair_ref, rot):
    pair_ref[...] = pair_of_panels(basis_ref, act_ref.shape[0])
    rotate(act_ref, pair_ref, rot, 0)
    ex_ref[...] = gradients(rg_ref[0], rot[0])


def second_kernel(*refs):
    act0_ref, act1_ref, rg_ref, mine_ref, other_ref, own0_ref, keep_ref, send_ref, sq_ref, rot, own_ref, ex_ref, pair_ref = refs
    e = lax.axis_index("ex")
    local, dirs, cols = own_ref.shape
    mid = dirs // 2
    rotate(act1_ref, mine_ref, rot, 0)
    pair_ref[...] = pair_of_panels(other_ref, act0_ref.shape[0])
    rotate(act0_ref, pair_ref, rot, 1)
    rotate(act1_ref, pair_ref, rot, 2)
    own_ref[0] = own0_ref[...]
    own_ref[1] = gradients(rg_ref[1], rot[0])
    for n in range(local):
        ex_ref[n] = gradients(rg_ref[n], rot[1 + n])
    here, there = (pl.ds(pl.multiple_of(x * mid, 8), mid) for x in (e, 1 - e))
    for n in range(local):
        for side, src in enumerate((own_ref, ex_ref)):
            keep_ref[n, side] = src[n, here, :]
            send_ref[n, side] = src[n, there, :]
    for side, src in enumerate((own_ref, ex_ref)):
        pair = e if side == 0 else 1 - e
        for h in range(2):
            for r in range(mid // 8):
                for c in range(cols // 128):
                    at = (pl.ds(h * mid + 8 * r, 8), pl.ds(128 * c, 128))
                    tile = src[0, at[0], at[1]] * src[0, at[0], at[1]]
                    for n in range(1, local):
                        tile += src[n, at[0], at[1]] * src[n, at[0], at[1]]
                    sq_ref[2 * (2 * (cols // 128) * r + (cols // 128) * pair + c) + h] = tile


def ex_gradients(act, rg, mine, other):
    local, dirs, tok = rg.shape
    width = act[0].shape[0]

    def cost(count):
        return pl.CostEstimate(
            flops=2 * count * tok * width * 256, transcendentals=0, bytes_accessed=2 * count * tok * width
        )

    own, pair = pl.pallas_call(
        first_kernel,
        in_specs=in_vmem(3),
        out_specs=in_vmem(2),
        out_shape=[pltpu.VMEM((dirs, 256), F32), pltpu.VMEM((256, width), BF16)],
        scratch_shapes=[pltpu.VMEM((1, 256, tok), BF16)],
        compiler_params=pltpu.CompilerParams(vmem_limit_bytes=16 << 20),
        cost_estimate=cost(1),
    )(act[0], rg, mine)
    return pl.pallas_call(
        second_kernel,
        in_specs=in_vmem(6),
        out_specs=in_vmem(3),
        out_shape=[
            pltpu.HBM((local, 2, dirs // 2, 256), F32),
            pltpu.HBM((local, 2, dirs // 2, 256), F32),
            pltpu.HBM((dirs * 512 // 1024, 8, 128), F32),
        ],
        scratch_shapes=[
            pltpu.VMEM((3, 256, tok), BF16),
            pltpu.VMEM((local, dirs, 256), F32),
            pltpu.VMEM((local, dirs, 256), F32),
            pltpu.VMEM((256, width), BF16),
        ],
        compiler_params=pltpu.CompilerParams(vmem_limit_bytes=16 << 20),
        cost_estimate=cost(3),
    )(*act, rg, pair, other, own)


def scale_kernel(lam_ref, keep_ref, got_ref, o_ref, inv, held, sem):
    e, i = lax.axis_index("ex"), pl.program_id(0)
    local = keep_ref.shape[0]
    tiles, across = lam_ref.shape[0] // 2, 4

    @pl.when(i == 0)
    def _():
        fetch = pltpu.make_async_copy(keep_ref, held, sem)
        fetch.start()
        damp = jnp.sum(jnp.sum(lam_ref[...], axis=0), keepdims=True) * (0.1 / lam_ref.size)
        for j in range(tiles):
            r, c = j // across, j % across
            inv[pl.ds(8 * r, 8), pl.ds(128 * c, 128)] = 1.0 / (lam_ref[2 * j + e] + damp)
        fetch.wait()

    for core in range(2):
        for j in range(local):
            for own in range(2):

                @pl.when((i == core * local + j) & (own == (e == core)))
                def _():
                    src = held if own else got_ref
                    for side in range(2):
                        at = pl.ds(256 * (core if side == 0 else 1 - core), 256)
                        o_ref[0, :, at] = src[j, side] * inv[:, at]


def scaled_rows(lam, keep, got):
    local, _, dirs, _ = keep.shape

    def whole(x):
        return pl.BlockSpec(x.shape, lambda i: (0,) * x.ndim)

    return pl.pallas_call(
        scale_kernel,
        grid=(2 * local,),
        in_specs=[whole(lam), pl.BlockSpec(memory_space=pl.ANY), whole(got)],
        out_specs=pl.BlockSpec((1, dirs, 512), lambda i: (i, 0, 0)),
        scratch_shapes=[pltpu.VMEM((dirs, 512), F32), pltpu.VMEM(keep.shape, F32), pltpu.SemaphoreType.DMA],
        out_shape=jax.ShapeDtypeStruct((2 * local, dirs, 512), F32),
        compiler_params=pltpu.CompilerParams(vmem_limit_bytes=8 << 20),
    )(lam, pltpu.with_memory_space_constraint(keep, pltpu.HBM), got)


def per_device(activations, out_grads, grad_basis, panel_store, owners, token_count):
    local, tok, width = activations.shape
    _, panels, half, pw = panel_store.shape
    n_basis, n_ex = lax.axis_size("basis"), lax.axis_size("ex")
    blocks = half // ROWS

    slots = panel_store.reshape(panels, blocks, ROWS, pw)
    sent = laid(owners, slots, n_basis)

    def to_chips(x):
        got = lax.all_to_all(x.reshape(-1, ROWS, pw), ("ex", "basis"), 0, 0, tiled=True)
        return got.reshape(2, n_basis, ROWS, pw)

    arrived = to_chips(sent)
    rg, act0, shared = early(owners, token_count, grad_basis, out_grads, activations)
    arrived, slots, act0, rg = lax.optimization_barrier((arrived, slots, act0, rg))
    act = [act0, activations[1].T]

    def second_panels(slots):
        second = to_chips(jnp.pad(slots[1::2], ((0, 0), (0, n_basis - blocks), (0, 0), (0, 0))))
        owner = owners[2 * lax.axis_index("ex") + 1]
        return lax.dynamic_index_in_dim(second, owner, 1, keepdims=False)

    second = lax.cond(
        shared[0] > 0, second_panels, lambda slots: jnp.zeros((2, ROWS, pw), slots.dtype), slots
    )
    mine = lax.all_to_all(picked(owners, arrived, second), "basis", 0, 0, tiled=True)

    swap = [(0, 1), (1, 0)]
    other = lax.ppermute(mine, "ex", swap)
    keep, send, squares = ex_gradients(act, rg, mine, other)
    got = lax.ppermute(send, "ex", swap)
    both = ("basis", "ex")
    parts = lax.all_to_all(squares, both, 0, 0, tiled=True)
    lam = jnp.sum(parts, axis=0, keepdims=True) * (1.0 / (local * n_basis * n_ex))
    lam = lax.all_to_all(jnp.broadcast_to(lam, parts.shape), both, 0, 0, tiled=True)
    return scaled_rows(lam, keep, got)


def solution(mesh):
    return jax.shard_map(
        per_device,
        mesh=mesh,
        in_specs=(
            P(("basis", "ex"), None, None),
            P(("basis", "ex"), None, None),
            P(),
            P("basis", None, "ex", None),
            P(),
            P(("basis", "ex")),
        ),
        out_specs=P("basis", "ex", None),
        check_vma=False,
    )
```
